32 devices in a mesh: seg: 4 (over y, x), blk: 8 (over z, core).
Axes of the slice: x: 2, y: 2, z: 4, core: 2. Of those that a mesh axis runs over, the one named last changes fastest.
Arguments:
- psi_init: float32 [4, 128, 128, 128], P('seg', 'blk'), may hold values from -6 to 6
- env_left: bfloat16 [4, 48, 8, 128, 128], P('seg', 'blk'), may hold values from -0.5 to 0.5
- env_right: bfloat16 [4, 48, 8, 128, 128], P('seg', 'blk'), may hold values from -0.5 to 0.5
- coef: float32 [4, 48, 128], P('seg', 'blk'), may hold values from -1.25 to 1.25
- source: int32 [4, 48, 128], P('seg', 'blk'), may hold values from 0 to 127
- right_sector: int32 [4, 16, 8], P('seg'), may hold values from 0 to 7, each once within a row
- sector_sizes: int32 [4, 2, 8], P('seg'), may hold values from 32 to 128, as said below
- step_size: float32 [4], P('seg'), may hold values from 0.2 to 0.6
Outputs:
- psi: float32 [4, 128, 128, 128], P('seg', 'blk')
- energy: float32 [4], P('seg')
- density: float32 [4, 1024, 128], P('seg', 'blk')
The draws below stay inside these ranges and needn't reach their ends.
Inputs may be any that keep to these rules, and one draw needn't show every extreme that they name: `sector_sizes`: in each row of 8 sizes one equals 128. `right_sector`: each row is a permutation of the sectors.
All inputs are finite; a program needn't handle non-finite values.
Results may differ from the reference program's by a relative error of at most 0.0018.
Values may be sent and summed in bfloat16 or wider, within the bound.
No kernel may reach another device: no remote copies, remote signals or barrier semaphores. Data moves between devices by JAX's collectives and lax.ppermute only.
A program may use at most 128 MiB of HBM per device.

```python
import math
import jax
import jax.numpy as jnp
from jax import lax

NSEC = 8
BS = 128
P_SIZE = 16
ITERS = 3
SEGS = 4
NB = 128
W = 48


def draw_sector_sizes(key, part):
    sizes = jax.random.randint(key, (SEGS, 2, NSEC), BS // 4, BS + 1)
    full_at = jax.random.randint(jax.random.fold_in(key, 7), (SEGS, 2, 1), 0, NSEC)
    labels = jnp.arange(NSEC)[None, None, :]
    return jnp.where(labels == full_at, BS, sizes).astype(jnp.int32)


def touch_ends(values, own_key, low, top_value):
    dims = values.shape
    index_at = [jax.random.randint(jax.random.fold_in(own_key, axis), (), 0, dims[axis]) for axis in range(len(dims))]
    values = values.at[tuple(index_at)].set(low)
    longest = dims.index(max(dims))
    index_at[longest] = (index_at[longest] + 1) % dims[longest]
    return values.at[tuple(index_at)].set(top_value)


def raised(entries, key, source, target, blocks, factor):
    owner, partner = [(jnp.arange(entries.shape[position]) // (entries.shape[position] // blocks)).reshape([-1 if axis == position else 1 for axis in range(entries.ndim)]) for position in (source, target)]
    chosen = jax.random.permutation(key, blocks)[partner]
    strong = (owner == chosen) | (owner == (partner + blocks // 2) % blocks)
    return jnp.where(strong, factor * entries, entries)


def level_of(rng, shape, pieces, smallest, top_value):
    factor_of = 1.0
    for position, blocks in pieces:
        heights = jax.random.uniform(jax.random.fold_in(jax.random.fold_in(rng, 6), position), (blocks,), jnp.float32, smallest / len(pieces), top_value / len(pieces))
        factor_of = factor_of * jnp.repeat(jnp.exp(heights), shape[position] // blocks).reshape((-1,) + (1,) * (len(shape) - 1 - position))
    return factor_of


def scatter_about(own_key, shape, scale, reach, shards=(), held_as=jnp.bfloat16):
    array = jax.random.normal(own_key, shape, jnp.float32) * scale
    if len(shards) > 0:
        array = level_of(own_key, shape, shards, -0.22, 0.18) * array
    return jnp.clip(array, min=-reach, max=reach).astype(held_as)


def noise_with(key, shape, deviation, reach, split, heavy, held_as=jnp.bfloat16):
    array = deviation * jax.random.normal(key, shape, jnp.float32)
    if split:
        array = array * level_of(key, shape, split, -0.22, 0.18)
    return jnp.clip(raised(array, jax.random.fold_in(key, 3), *heavy), -reach, reach).astype(held_as)


def setup_inputs(seed: int = 0) -> dict:
    key_of = jax.random.split(jax.random.key(seed), 9)
    psi_init = scatter_about(key_of[0], (SEGS, NB, BS, BS), 1.0, 6.0, ((0, 4), (1, 8)), jnp.float32)
    env_left = scatter_about(key_of[1], (SEGS, W, NSEC, BS, BS), BS ** -0.5, 0.5, ((0, 4), (1, 8)))
    env_right = scatter_about(key_of[2], (SEGS, W, NSEC, BS, BS), BS ** -0.5, 0.5, ((0, 4), (1, 8)))
    coef = noise_with(key_of[3], (SEGS, W, NB), W ** -0.5, 1.25, ((0, 4), (1, 8)), (1, 2, 8, 2.0), jnp.float32)
    source = touch_ends(jax.random.randint(key_of[4], (SEGS, W, NB), 0, NB), jax.random.fold_in(key_of[4], 1), 0, NB - 1).astype(jnp.int32)
    right_sector = jax.vmap(lambda own: jax.random.permutation(own, NSEC))(jax.random.split(key_of[5], SEGS * P_SIZE)).reshape((SEGS, P_SIZE, NSEC)).astype(jnp.int32)
    sector_sizes = draw_sector_sizes(jax.random.fold_in(key_of[8], 71), 0)
    step_size = jnp.clip(jnp.exp(math.log(0.6) - 1.0986123 * jax.random.uniform(key_of[7], (SEGS,), jnp.float32) ** level_of(key_of[7], (SEGS,), ((0, 4),), -0.2, 0.2)), 0.2, 0.6)
    return {"psi_init": psi_init, "env_left": env_left, "env_right": env_right, "coef": coef, "source": source, "right_sector": right_sector, "sector_sizes": sector_sizes, "step_size": step_size}


def block_mask(sizes, right_ids):
    indices = jnp.arange(NB)
    left_ids = indices % NSEC
    positions = jnp.arange(BS)
    row_live = positions[None, :] < sizes[0][left_ids][:, None]
    col_live = positions[None, :] < sizes[1][right_ids][:, None]
    return (row_live[:, :, None] & col_live[:, None, :]).astype(jnp.float32)

def apply_operator(vector_bf, left_env, right_env, weights, sources, right_ids):
    left_ids = jnp.arange(NB) % NSEC

    def channel(accum, inputs):
        left_one, right_one, source_one, weight_one = inputs
        picked = vector_bf[source_one].astype(jnp.float32)
        left_mats = left_one[left_ids].astype(jnp.float32)
        middle = jnp.einsum('nay,nyb->nab', left_mats, picked, precision=lax.Precision.HIGHEST).astype(jnp.bfloat16)
        right_mats = right_one[right_ids].astype(jnp.float32)
        result = jnp.einsum('nab,ncb->nac', middle.astype(jnp.float32), right_mats, precision=lax.Precision.HIGHEST)
        return (accum + weight_one[:, None, None] * result, None)
    initial = jnp.zeros((NB, BS, BS), jnp.float32)
    summed, _ = lax.scan(channel, initial, (left_env, right_env, sources, weights))
    return summed

def gram_parts(vector, right_ids):
    left_ids = jnp.arange(NB) % NSEC
    gram_left = jnp.einsum('nxb,nyb->nxy', vector, vector, precision=lax.Precision.HIGHEST)
    gram_right = jnp.einsum('nax,nay->nxy', vector, vector, precision=lax.Precision.HIGHEST)
    labels = jnp.arange(NSEC)
    one_left = (left_ids[:, None] == labels[None, :]).astype(jnp.float32)
    one_right = (right_ids[:, None] == labels[None, :]).astype(jnp.float32)
    left_rho = jnp.einsum('ns,nxy->sxy', one_left, gram_left, precision=lax.Precision.HIGHEST).reshape(NSEC * BS, BS)
    right_rho = jnp.einsum('ns,nxy->sxy', one_right, gram_right, precision=lax.Precision.HIGHEST).reshape(NSEC * BS, BS)
    return (left_rho, right_rho)

def reference(psi_init, env_left, env_right, coef, source, right_sector, sector_sizes, step_size):
    cells_total = float(NB * BS * BS)
    vectors = []
    quotients = []
    lefts = []
    rights = []
    for segment in range(SEGS):
        right_ids = right_sector[segment].reshape(NB)
        live = block_mask(sector_sizes[segment], right_ids)
        vector = psi_init[segment] * live
        quotient = jnp.zeros((), jnp.float32)
        step_len = step_size[segment]
        for iteration in range(ITERS):
            vector_bf = vector.astype(jnp.bfloat16)
            applied = apply_operator(vector_bf, env_left[segment], env_right[segment], coef[segment], source[segment], right_ids) * live
            square_sum = jnp.sum(vector * vector)
            cross_sum = jnp.sum(vector * applied)
            image_sum = jnp.sum(applied * applied)
            quotient = cross_sum / square_sum
            new_norm = square_sum + step_len * step_len * (image_sum - quotient * quotient * square_sum)
            vector = (vector - step_len * (applied - quotient * vector)) * jnp.sqrt(cells_total / new_norm)
        left_rho, right_rho = gram_parts(vector, right_ids)
        vectors.append(vector)
        quotients.append(quotient)
        lefts.append(left_rho)
        rights.append(right_rho)
    densities = []
    for segment in range(SEGS):
        if segment > 0:
            combined = lefts[segment] + rights[segment - 1]
        else:
            combined = lefts[segment]
        densities.append(combined / float(P_SIZE * BS))
    return (jnp.stack(vectors), jnp.stack(quotients), jnp.stack(densities))
```

```python
import functools

import jax
import jax.numpy as jnp
from jax import lax
from jax.experimental import pallas as pl
from jax.experimental.pallas import tpu as pltpu
from jax.sharding import PartitionSpec as P

NSEC = 8
BS = 128
P_SIZE = 16
ITERS = 3
NB = 128


def shifted_2(block, axis, distance):
    devices = range(lax.axis_size(axis))
    route = [(i - distance, i) for i in devices if i - distance in devices]
    return lax.ppermute(block, axis, route)


def block_mask(indices, sizes, right_flat):
    left_ids = indices % NSEC
    right_ids = jnp.take(right_flat, indices)
    positions = jnp.arange(BS, dtype=jnp.int32)
    row_live = positions[None, :] < jnp.take(sizes[0], left_ids)[:, None]
    col_live = positions[None, :] < jnp.take(sizes[1], right_ids)[:, None]
    return (row_live[:, :, None] & col_live[:, None, :]).astype(jnp.float32)


def apply_terms(full_bf, indices, left_env, right_env, weights, sources, right_flat):
    left_ids = indices % NSEC
    right_ids = jnp.take(right_flat, indices)

    def channel(accum, inputs):
        left_one, right_one, source_one, weight_one = inputs
        picked = jnp.take(full_bf, jnp.take(source_one, indices), axis=0)
        left_mats = jnp.take(left_one, left_ids, axis=0)
        middle = jnp.einsum(
            "nay,nyb->nab", left_mats, picked, preferred_element_type=jnp.float32
        ).astype(jnp.bfloat16)
        right_mats = jnp.take(right_one, right_ids, axis=0)
        result = jnp.einsum("nab,ncb->nac", middle, right_mats, preferred_element_type=jnp.float32)
        scaled = jnp.take(weight_one, indices)
        return (accum + scaled[:, None, None] * result, None)

    initial = jnp.zeros((indices.shape[0], BS, BS), jnp.float32)
    summed, _ = lax.scan(channel, initial, (left_env, right_env, sources, weights))
    return summed


def gram_parts(vector, indices, right_flat):
    left_ids = indices % NSEC
    right_ids = jnp.take(right_flat, indices)
    gram_left = jnp.einsum("nxb,nyb->nxy", vector, vector, precision=lax.Precision.HIGHEST)
    gram_right = jnp.einsum("nax,nay->nxy", vector, vector, precision=lax.Precision.HIGHEST)
    labels = jnp.arange(NSEC, dtype=jnp.int32)
    one_left = (left_ids[:, None] == labels[None, :]).astype(jnp.float32)
    one_right = (right_ids[:, None] == labels[None, :]).astype(jnp.float32)
    left_rho = jnp.einsum(
        "ns,nxy->sxy", one_left, gram_left, precision=lax.Precision.HIGHEST
    ).reshape(NSEC * BS, BS)
    right_rho = jnp.einsum(
        "ns,nxy->sxy", one_right, gram_right, precision=lax.Precision.HIGHEST
    ).reshape(NSEC * BS, BS)
    return (left_rho, right_rho)


def update_vector(current, applied, square_sum, cross_sum, image_sum, step_len, cells_total):
    quotient = cross_sum / square_sum
    new_norm = square_sum + step_len * step_len * (image_sum - quotient * quotient * square_sum)
    updated = (current - step_len * (applied - quotient * current)) * jnp.sqrt(
        cells_total / new_norm
    )
    return (updated, quotient)


def on_device_general(psi_init, env_left, env_right, coef, source, right_sector, sector_sizes, step_size):
    left_env = env_left[0]
    right_env = env_right[0]
    weights = coef[0]
    sources = source[0]
    right_flat = right_sector[0].reshape(NB)
    sizes = sector_sizes[0]
    step_len = step_size[0]
    own_count = psi_init.shape[1]
    cells_total = float(NB * BS * BS)
    own_ids = lax.axis_index("blk") * own_count + jnp.arange(own_count, dtype=jnp.int32)
    own_live = block_mask(own_ids, sizes, right_flat)
    current = psi_init[0] * own_live
    quotient = jnp.zeros((), jnp.float32)
    for iteration in range(ITERS):
        full_bf = lax.all_gather(current.astype(jnp.bfloat16), "blk", axis=0, tiled=True)

        def partial_terms(begin_row, row_count, full_bf=full_bf):
            indices = jnp.arange(row_count, dtype=jnp.int32)
            return apply_terms(full_bf, indices, left_env, right_env, weights, sources, right_flat)

        applied = (
            lax.psum_scatter(
                partial_terms(jnp.int32(0), own_count * lax.axis_size("blk")),
                "blk",
                scatter_dimension=0,
                tiled=True,
            )
            * own_live
        )
        square_sum, cross_sum, image_sum = lax.psum(
            (jnp.sum(current * current), jnp.sum(current * applied), jnp.sum(applied * applied)),
            "blk",
        )
        current, quotient = update_vector(
            current, applied, square_sum, cross_sum, image_sum, step_len, cells_total
        )
    left_part, right_part = gram_parts(current, own_ids, right_flat)
    left_rows, right_rows = (
        lax.psum_scatter(left_part, "blk", scatter_dimension=0, tiled=True),
        lax.psum_scatter(right_part, "blk", scatter_dimension=0, tiled=True),
    )
    shifted = shifted_2(right_rows, "seg", 1)
    density = (left_rows + shifted) / float(P_SIZE * BS)
    return (current[None], quotient.reshape(1), density[None])


BF = jnp.bfloat16
F32 = jnp.float32
MIB = 1 << 20
TOP = 32767.0
EXP_ROWS = 16
ROWS_ROWS = (((1,), (1,)), ((), ()))
COLS_COLS = (((0,), (0,)), ((), ()))
SMEM = pl.BlockSpec(memory_space=pltpu.SMEM)
VMEM = pl.BlockSpec(memory_space=pltpu.VMEM)


def terms_kernel(
    coded, turned, unroll, place, coef_a, coef_b, from_a, from_b, inverse, full,
    left_a, left_b, right_a, right_b, out, middle,
):
    halves = ((coef_a, from_a, left_a, right_a), (coef_b, from_b, left_b, right_b))
    count = left_a.shape[0]
    base = place[0] * (2 * NSEC)

    def first(a):
        for half, (_, sources, left, _) in enumerate(halves):
            for k in range(count):
                one = full[sources[k, base + a]]
                two = full[sources[k, base + NSEC + a]]
                if turned:
                    both = jnp.concatenate([one, two], axis=0)
                    product = lax.dot_general(
                        left[k, a], both, ROWS_ROWS, preferred_element_type=F32
                    )
                else:
                    both = jnp.concatenate([one, two], axis=1)
                    product = jnp.dot(left[k, a], both, preferred_element_type=F32)
                product = product.astype(BF)
                middle[half * count + k, 0, a] = product[:, :BS]
                middle[half * count + k, 1, a] = product[:, BS:]

    def second(b):
        picked = [inverse[place[0] * 2 + t, b] for t in range(2)]
        sums = [None, None]
        for half, (weights, _, _, right) in enumerate(halves):
            for k in range(count):
                both = jnp.concatenate(
                    [middle[half * count + k, t, picked[t]] for t in range(2)], axis=0
                )
                product = lax.dot_general(right[k, b], both, ROWS_ROWS, preferred_element_type=F32)
                for t in range(2):
                    term = product[:, t * BS : (t + 1) * BS] * weights[k, base + t * NSEC + picked[t]]
                    sums[t] = term if sums[t] is None else sums[t] + term
        for t in range(2):
            index = t * NSEC + picked[t]
            if not coded:
                out[index] = sums[t]
                continue
            most = jnp.max(jnp.abs(sums[t]), axis=(0, 1), keepdims=True)
            power = jnp.clip(jnp.ceil(jnp.log2(jnp.maximum(most, 1e-30) / TOP)), -100.0, 100.0)
            whole = jnp.clip(jnp.round(sums[t] * jnp.exp2(-power)), -TOP, TOP)
            rows = pl.ds(pl.multiple_of(index * BS, BS), BS)
            out[rows, :] = whole.astype(jnp.int32).astype(jnp.int16)
            last = 2 * NSEC * BS
            here = lax.broadcasted_iota(jnp.int32, (EXP_ROWS, BS), 0) == index
            old = out[last : last + EXP_ROWS, :].astype(jnp.int32)
            new = jnp.broadcast_to(power.astype(jnp.int32), (EXP_ROWS, BS))
            out[last : last + EXP_ROWS, :] = jnp.where(here, new, old).astype(jnp.int16)

    def run(step):
        def several(i, carry):
            for j in range(unroll):
                step(i * unroll + j)
            return carry

        lax.fori_loop(0, NSEC // unroll, several, 0)

    run(first)
    run(second)


def terms(coded, turned, place, tables, full, envs):
    channels = 2 * envs[0].shape[0]
    blocks = 2 * NSEC
    if coded:
        shape = jax.ShapeDtypeStruct((blocks * BS + EXP_ROWS, BS), jnp.int16)
    else:
        shape = jax.ShapeDtypeStruct((blocks, BS, BS), F32)
    return pl.pallas_call(
        functools.partial(terms_kernel, coded, turned, 2),
        out_shape=shape,
        in_specs=[SMEM] * 6 + [VMEM] * 5,
        out_specs=VMEM,
        scratch_shapes=[pltpu.VMEM((channels, 2, NSEC, BS, BS), BF)],
        compiler_params=pltpu.CompilerParams(vmem_limit_bytes=24 * MIB),
        cost_estimate=pl.CostEstimate(
            flops=channels * blocks * 4 * BS**3, bytes_accessed=8 * MIB, transcendentals=0
        ),
    )(place, *tables, full, *envs)


def combine_kernel(place, sizes, labels, own, *refs):
    coded, current, applied, sums = refs[:-3], refs[-3], refs[-2], refs[-1]
    blocks = own.shape[0]
    down = lax.broadcasted_iota(jnp.int32, (BS, BS), 0)
    across = lax.broadcasted_iota(jnp.int32, (BS, BS), 1)
    totals = [jnp.zeros((8, BS), F32) for _ in range(3)]
    for i in range(blocks):
        t, a = i // NSEC, i % NSEC
        value = own[i]
        for one in coded:
            power = one[blocks * BS : blocks * BS + EXP_ROWS, :].astype(jnp.int32).astype(F32)
            scale = jnp.exp2(power[i : i + 1, :])
            value = value + one[i * BS : (i + 1) * BS, :].astype(jnp.int32).astype(F32) * scale
        live = (across < sizes[0, a]) & (down < sizes[1, labels[place[0] * 2 + t, a]])
        value = jnp.where(live, value, 0.0)
        applied[i] = value
        old = current[i]
        for n, terms_of in enumerate((old * old, old * value, value * value)):
            totals[n] = totals[n] + jnp.sum(terms_of.reshape(BS // 8, 8, BS), axis=0)
    for n in range(3):
        sums[n] = totals[n]


def combine(place, sizes, labels, own, coded, current):
    return pl.pallas_call(
        combine_kernel,
        out_shape=(
            jax.ShapeDtypeStruct(own.shape, F32),
            jax.ShapeDtypeStruct((3, 8, BS), F32),
        ),
        in_specs=[SMEM] * 3 + [VMEM] * (2 + len(coded)),
        out_specs=(VMEM, VMEM),
        compiler_params=pltpu.CompilerParams(vmem_limit_bytes=16 * MIB),
        cost_estimate=pl.CostEstimate(flops=10 * own.size, bytes_accessed=4 * MIB, transcendentals=0),
    )(place, sizes, labels, own, *coded, current)


def finish_kernel(place, scalars, inverse, current, applied, psi, left, right):
    keep, take = scalars[0], scalars[1]
    blocks = current.shape[0]
    vals = [keep * current[i] - take * applied[i] for i in range(blocks)]
    for i in range(blocks):
        psi[i] = vals[i].T
        applied[i] = vals[i]

    def gram(dims, one, two):
        kw = dict(precision=lax.Precision.HIGHEST, preferred_element_type=F32)
        return lax.dot_general(one, one, dims, **kw) + lax.dot_general(two, two, dims, **kw)

    for a in range(NSEC):
        left[a] = gram(COLS_COLS, vals[a], vals[NSEC + a])
    for b in range(NSEC):
        one = applied[inverse[place[0] * 2, b]]
        two = applied[NSEC + inverse[place[0] * 2 + 1, b]]
        right[b] = gram(ROWS_ROWS, one, two)


def finish(place, scalars, inverse, current, applied):
    def kernel(place, scalars, inverse, current, applied, psi, left, right, hold):
        for i in range(current.shape[0]):
            hold[i] = applied[i]
        finish_kernel(place, scalars, inverse, current, hold, psi, left, right)

    rho = jax.ShapeDtypeStruct((NSEC, BS, BS), F32)
    return pl.pallas_call(
        kernel,
        out_shape=(jax.ShapeDtypeStruct(current.shape, F32), rho, rho),
        in_specs=[SMEM] * 3 + [VMEM] * 2,
        out_specs=(VMEM,) * 3,
        scratch_shapes=[pltpu.VMEM(current.shape, F32)],
        compiler_params=pltpu.CompilerParams(vmem_limit_bytes=24 * MIB),
    )(place, scalars, inverse, current, applied)


def on_device_paired(psi_init, env_left, env_right, coef, source, right_sector, sector_sizes, step_size):
    count = lax.axis_size("blk")
    line = count // 2
    me = lax.axis_index("blk")
    swap = [(i, i ^ 1) for i in range(count)]
    labels = right_sector[0]
    sizes = sector_sizes[0]
    step_len = step_size[0]
    cells_total = float(NB * BS * BS)

    def moved(x, by):
        route = [(i, (i + 2 * by) % count) for i in range(count)]
        return lax.ppermute(x, "blk", route)

    mine = (env_left[0], env_right[0], coef[0], source[0])
    other = tuple(lax.ppermute(x, "blk", swap) for x in mine)
    envs = (mine[0], other[0], mine[1], other[1])
    sector = jnp.arange(NSEC, dtype=jnp.int32)
    inverse = jnp.sum(
        jnp.where(labels[:, :, None] == sector[None, None, :], sector[None, :, None], 0), axis=1
    ).astype(jnp.int32)
    tables = (mine[2], other[2], mine[3], other[3], inverse)
    places = [((me + 2 * by) % count).astype(jnp.int32).reshape(1) for by in range(line)]
    order = sorted(range(1, line), key=lambda by: -min(by, line - by))

    own_count = psi_init.shape[1]
    own_ids = me * own_count + jnp.arange(own_count, dtype=jnp.int32)
    start = psi_init[0] * block_mask(own_ids, sizes, labels.reshape(NB))
    current = jnp.swapaxes(start, 1, 2)
    half = start.astype(BF)
    for iteration in range(ITERS):
        full = lax.all_gather(half, "blk", axis=0, tiled=True)
        turned = iteration > 0
        arrived = []
        for by in order:
            arrived.append(moved(terms(True, turned, places[by], tables, full, envs), by))
        own = terms(False, turned, places[0], tables, full, envs)
        applied, sums = combine(places[0], sizes, labels, own, arrived, current)
        square_sum, cross_sum, image_sum = lax.psum(jnp.sum(sums, axis=(1, 2)), "blk")
        quotient = cross_sum / square_sum
        new_norm = square_sum + step_len * step_len * (image_sum - quotient * quotient * square_sum)
        scale = jnp.sqrt(cells_total / new_norm)
        keep = (1.0 + step_len * quotient) * scale
        take = step_len * scale
        if iteration < ITERS - 1:
            current = keep * current - take * applied
            half = current.astype(BF)
    psi, left_part, right_part = finish(
        places[0], jnp.stack([keep, take]), inverse, current, applied
    )
    both = jnp.concatenate([left_part, right_part], axis=1).reshape(2 * NSEC * BS, BS)
    both = lax.psum_scatter(both, "blk", scatter_dimension=0, tiled=True)
    shifted = shifted_2(both[BS:], "seg", 1)
    density = (both[:BS] + shifted) / float(P_SIZE * BS)
    return (psi[None], quotient.reshape(1), density[None])


def solution(mesh):
    in_specs = (
        P("seg", "blk", None, None),
        P("seg", "blk", None, None, None),
        P("seg", "blk", None, None, None),
        P("seg", "blk", None),
        P("seg", "blk", None),
        P("seg", None, None),
        P("seg", None, None),
        P("seg"),
    )
    out_specs = (P("seg", "blk", None, None), P("seg"), P("seg", "blk", None))
    paired = NB // mesh.shape["blk"] == 2 * NSEC and mesh.shape["blk"] % 2 == 0
    return jax.shard_map(
        on_device_paired if paired else on_device_general,
        mesh=mesh,
        in_specs=in_specs,
        out_specs=out_specs,
        check_vma=False,
    )
```

```python
import functools

import jax
import jax.numpy as jnp
from jax import lax
from jax.experimental import pallas as pl
from jax.experimental.pallas import tpu as pltpu
from jax.sharding import PartitionSpec as P

NSEC = 8
BS = 128
P_SIZE = 16
ITERS = 3
NB = 128


def shifted_2(block, axis, distance):
    devices = range(lax.axis_size(axis))
    route = [(i - distance, i) for i in devices if i - distance in devices]
    return lax.ppermute(block, axis, route)


def block_mask(indices, sizes, right_flat):
    left_ids = indices % NSEC
    right_ids = jnp.take(right_flat, indices)
    positions = jnp.arange(BS, dtype=jnp.int32)
    row_live = positions[None, :] < jnp.take(sizes[0], left_ids)[:, None]
    col_live = positions[None, :] < jnp.take(sizes[1], right_ids)[:, None]
    return (row_live[:, :, None] & col_live[:, None, :]).astype(jnp.float32)


def apply_terms(full_bf, indices, left_env, right_env, weights, sources, right_flat):
    left_ids = indices % NSEC
    right_ids = jnp.take(right_flat, indices)

    def channel(accum, inputs):
        left_one, right_one, source_one, weight_one = inputs
        picked = jnp.take(full_bf, jnp.take(source_one, indices), axis=0)
        left_mats = jnp.take(left_one, left_ids, axis=0)
        middle = jnp.einsum(
            "nay,nyb->nab", left_mats, picked, preferred_element_type=jnp.float32
        ).astype(jnp.bfloat16)
        right_mats = jnp.take(right_one, right_ids, axis=0)
        result = jnp.einsum("nab,ncb->nac", middle, right_mats, preferred_element_type=jnp.float32)
        scaled = jnp.take(weight_one, indices)
        return (accum + scaled[:, None, None] * result, None)

    initial = jnp.zeros((indices.shape[0], BS, BS), jnp.float32)
    summed, _ = lax.scan(channel, initial, (left_env, right_env, sources, weights))
    return summed


def gram_parts(vector, indices, right_flat):
    left_ids = indices % NSEC
    right_ids = jnp.take(right_flat, indices)
    gram_left = jnp.einsum("nxb,nyb->nxy", vector, vector, precision=lax.Precision.HIGHEST)
    gram_right = jnp.einsum("nax,nay->nxy", vector, vector, precision=lax.Precision.HIGHEST)
    labels = jnp.arange(NSEC, dtype=jnp.int32)
    one_left = (left_ids[:, None] == labels[None, :]).astype(jnp.float32)
    one_right = (right_ids[:, None] == labels[None, :]).astype(jnp.float32)
    left_rho = jnp.einsum(
        "ns,nxy->sxy", one_left, gram_left, precision=lax.Precision.HIGHEST
    ).reshape(NSEC * BS, BS)
    right_rho = jnp.einsum(
        "ns,nxy->sxy", one_right, gram_right, precision=lax.Precision.HIGHEST
    ).reshape(NSEC * BS, BS)
    return (left_rho, right_rho)


def update_vector(current, applied, square_sum, cross_sum, image_sum, step_len, cells_total):
    quotient = cross_sum / square_sum
    new_norm = square_sum + step_len * step_len * (image_sum - quotient * quotient * square_sum)
    updated = (current - step_len * (applied - quotient * current)) * jnp.sqrt(
        cells_total / new_norm
    )
    return (updated, quotient)


def on_device_general(psi_init, env_left, env_right, coef, source, right_sector, sector_sizes, step_size):
    left_env = env_left[0]
    right_env = env_right[0]
    weights = coef[0]
    sources = source[0]
    right_flat = right_sector[0].reshape(NB)
    sizes = sector_sizes[0]
    step_len = step_size[0]
    own_count = psi_init.shape[1]
    cells_total = float(NB * BS * BS)
    own_ids = lax.axis_index("blk") * own_count + jnp.arange(own_count, dtype=jnp.int32)
    own_live = block_mask(own_ids, sizes, right_flat)
    current = psi_init[0] * own_live
    quotient = jnp.zeros((), jnp.float32)
    for iteration in range(ITERS):
        full_bf = lax.all_gather(current.astype(jnp.bfloat16), "blk", axis=0, tiled=True)

        def partial_terms(begin_row, row_count, full_bf=full_bf):
            indices = jnp.arange(row_count, dtype=jnp.int32)
            return apply_terms(full_bf, indices, left_env, right_env, weights, sources, right_flat)

        applied = (
            lax.psum_scatter(
                partial_terms(jnp.int32(0), own_count * lax.axis_size("blk")),
                "blk",
                scatter_dimension=0,
                tiled=True,
            )
            * own_live
        )
        square_sum, cross_sum, image_sum = lax.psum(
            (jnp.sum(current * current), jnp.sum(current * applied), jnp.sum(applied * applied)),
            "blk",
        )
        current, quotient = update_vector(
            current, applied, square_sum, cross_sum, image_sum, step_len, cells_total
        )
    left_part, right_part = gram_parts(current, own_ids, right_flat)
    left_rows, right_rows = (
        lax.psum_scatter(left_part, "blk", scatter_dimension=0, tiled=True),
        lax.psum_scatter(right_part, "blk", scatter_dimension=0, tiled=True),
    )
    shifted = shifted_2(right_rows, "seg", 1)
    density = (left_rows + shifted) / float(P_SIZE * BS)
    return (current[None], quotient.reshape(1), density[None])


BF = jnp.bfloat16
F32 = jnp.float32
MIB = 1 << 20
TOP = 32767.0
EXP_ROWS = 16
UNROLL = 2
ROWS_ROWS = (((1,), (1,)), ((), ()))
COLS_COLS = (((0,), (0,)), ((), ()))
SMEM = pl.BlockSpec(memory_space=pltpu.SMEM)
VMEM = pl.BlockSpec(memory_space=pltpu.VMEM)


def parameters(mib):
    return pltpu.CompilerParams(vmem_limit_bytes=mib * MIB)


def terms_kernel(
    turned, unroll, place, coef_a, coef_b, from_a, from_b, inverse, full,
    left_a, left_b, right_a, right_b, out_a, out_b, middle,
):
    halves = ((coef_a, from_a, left_a, right_a), (coef_b, from_b, left_b, right_b))
    count = left_a.shape[0]
    base = place[0] * (2 * NSEC)

    def first(a):
        for half, (_, sources, left, _) in enumerate(halves):
            for k in range(count):
                one = full[sources[k, base + a]]
                two = full[sources[k, base + NSEC + a]]
                if turned:
                    both = jnp.concatenate([one, two], axis=0)
                    product = lax.dot_general(
                        left[k, a], both, ROWS_ROWS, preferred_element_type=F32
                    )
                else:
                    both = jnp.concatenate([one, two], axis=1)
                    product = jnp.dot(left[k, a], both, preferred_element_type=F32)
                product = product.astype(BF)
                middle[half * count + k, 0, a] = product[:, :BS]
                middle[half * count + k, 1, a] = product[:, BS:]

    def second(b):
        picked = [inverse[place[0] * 2 + t, b] for t in range(2)]
        sums = [None, None]
        for half, (weights, _, _, right) in enumerate(halves):
            for k in range(count):
                both = jnp.concatenate(
                    [middle[half * count + k, t, picked[t]] for t in range(2)], axis=0
                )
                product = lax.dot_general(right[k, b], both, ROWS_ROWS, preferred_element_type=F32)
                for t in range(2):
                    term = product[:, t * BS : (t + 1) * BS] * weights[k, base + t * NSEC + picked[t]]
                    sums[t] = term if sums[t] is None else sums[t] + term
        out_a[picked[0]] = sums[0]
        out_b[picked[1]] = sums[1]

    def run(step):
        def several(i, carry):
            for j in range(unroll):
                step(i * unroll + j)
            return carry

        lax.fori_loop(0, NSEC // unroll, several, 0)

    run(first)
    run(second)


def terms(turned, place, tables, full, envs):
    channels = 2 * envs[0].shape[0]
    half = jax.ShapeDtypeStruct((NSEC, BS, BS), F32)
    return pl.pallas_call(
        functools.partial(terms_kernel, turned, UNROLL),
        out_shape=(half, half),
        in_specs=[SMEM] * 6 + [VMEM] * 5,
        out_specs=(VMEM, VMEM),
        scratch_shapes=[pltpu.VMEM((channels, 2, NSEC, BS, BS), BF)],
        compiler_params=parameters(24),
        cost_estimate=pl.CostEstimate(
            flops=channels * NSEC * 8 * BS**3, bytes_accessed=8 * MIB, transcendentals=0
        ),
    )(place, *tables, full, *envs)


CODED = jax.ShapeDtypeStruct((NSEC * BS + EXP_ROWS, BS), jnp.int16)


def decoded(ref, index):
    power = ref[NSEC * BS : NSEC * BS + EXP_ROWS, :].astype(jnp.int32).astype(F32)
    value = ref[index * BS : (index + 1) * BS, :].astype(jnp.int32).astype(F32)
    return value * jnp.exp2(power[index : index + 1, :])


def relay_kernel(*refs):
    own, out = refs[-2], refs[-1]
    rows = lax.broadcasted_iota(jnp.int32, (EXP_ROWS, BS), 0)
    powers = jnp.zeros((EXP_ROWS, BS), jnp.int32)
    for i in range(NSEC):
        value = own[i]
        for ref in refs[:-2]:
            value = value + decoded(ref, i)
        most = jnp.max(jnp.max(jnp.abs(value), axis=0, keepdims=True), axis=1, keepdims=True)
        power = jnp.clip(jnp.ceil(jnp.log2(jnp.maximum(most, 1e-30) / TOP)), -100.0, 100.0)
        whole = jnp.clip(jnp.round(value * jnp.exp2(-power)), -TOP, TOP)
        out[i * BS : (i + 1) * BS, :] = whole.astype(jnp.int32).astype(jnp.int16)
        powers = jnp.where(rows == i, power.astype(jnp.int32), powers)
    out[NSEC * BS : NSEC * BS + EXP_ROWS, :] = powers.astype(jnp.int16)


def relay(arrived, own):
    return pl.pallas_call(
        relay_kernel,
        out_shape=CODED,
        in_specs=[VMEM] * (len(arrived) + 1),
        out_specs=VMEM,
        compiler_params=parameters(8),
        cost_estimate=pl.CostEstimate(flops=10 * own.size, bytes_accessed=MIB, transcendentals=0),
    )(*arrived, own)


def assemble_kernel(*refs):
    pieces, out, sems = refs[:-2], refs[-2], refs[-1]
    size = pieces[0].shape[0]
    copies = [
        pltpu.make_async_copy(piece, out.at[pl.ds(n * size, size)], sems.at[n])
        for n, piece in enumerate(pieces)
    ]
    for copy in copies:
        copy.start()
    for copy in copies:
        copy.wait()


def assemble(pieces):
    total = sum(piece.shape[0] for piece in pieces)
    return pl.pallas_call(
        assemble_kernel,
        out_shape=jax.ShapeDtypeStruct((total, BS, BS), BF),
        in_specs=[pl.BlockSpec(memory_space=pl.ANY)] * len(pieces),
        out_specs=VMEM,
        scratch_shapes=[pltpu.SemaphoreType.DMA((len(pieces),))],
        compiler_params=parameters(8),
    )(*pieces)


def combine_kernel(half, place, sizes, labels, *refs):
    before, (own, coded, current, applied, sums) = refs[:-5], refs[-5:]
    down = lax.broadcasted_iota(jnp.int32, (BS, BS), 0)
    across = lax.broadcasted_iota(jnp.int32, (BS, BS), 1)
    totals = [jnp.zeros((8, BS), F32) for _ in range(3)]
    for a in range(NSEC):
        live = (across < sizes[0, a]) & (down < sizes[1, labels[place[0] * 2 + half, a]])
        value = jnp.where(live, own[a] + decoded(coded, a), 0.0)
        applied[a] = value
        old = current[a]
        for n, terms_of in enumerate((old * old, old * value, value * value)):
            totals[n] = totals[n] + jnp.sum(terms_of.reshape(BS // 8, 8, BS), axis=0)
    rows = lax.broadcasted_iota(jnp.int32, (8, BS), 0)
    result = jnp.zeros((8, BS), F32)
    for n in range(3):
        result = jnp.where(rows == n, jnp.sum(totals[n], axis=0, keepdims=True), result)
    for ref in before:
        result = result + ref[...]
    sums[...] = result


def combine(half, place, sizes, labels, before, own, coded, current):
    return pl.pallas_call(
        functools.partial(combine_kernel, half),
        out_shape=(
            jax.ShapeDtypeStruct(own.shape, F32),
            jax.ShapeDtypeStruct((8, BS), F32),
        ),
        in_specs=[SMEM] * 3 + [VMEM] * (3 + len(before)),
        out_specs=(VMEM, VMEM),
        compiler_params=parameters(8),
        cost_estimate=pl.CostEstimate(flops=10 * own.size, bytes_accessed=2 * MIB, transcendentals=0),
    )(place, sizes, labels, *before, own, coded, current)


def factors(parts, step_len, cells_total):
    total = (parts[0][...] + parts[2][...]) + (parts[1][...] + parts[3][...])
    total = jnp.sum(total, axis=1, keepdims=True)
    square_sum, cross_sum, image_sum = total[0:1], total[1:2], total[2:3]
    quotient = cross_sum / square_sum
    new_norm = square_sum + step_len * step_len * (image_sum - quotient * quotient * square_sum)
    scale = jnp.sqrt(cells_total / new_norm)
    return (1.0 + step_len * quotient) * scale, step_len * scale, quotient


def update_kernel(cells_total, step_len, *refs):
    parts, (current, applied, out, narrow) = refs[:-4], refs[-4:]
    keep, take, _ = factors(parts, step_len[0], cells_total)
    for i in range(current.shape[0]):
        value = keep * current[i] - take * applied[i]
        out[i] = value
        narrow[i] = value.astype(BF)


def update(cells_total, step_size, parts, current, applied):
    return pl.pallas_call(
        functools.partial(update_kernel, cells_total),
        out_shape=(
            jax.ShapeDtypeStruct(current.shape, F32),
            jax.ShapeDtypeStruct(current.shape, BF),
        ),
        in_specs=[SMEM] + [VMEM] * (len(parts) + 2),
        out_specs=(VMEM, VMEM),
        compiler_params=parameters(8),
    )(step_size, *parts, current, applied)


def finish_kernel(cells_total, place, step_len, inverse, *refs):
    parts = refs[:4]
    current_a, current_b, applied_a, applied_b, psi, energy, keep_rho, give_rho, hold = refs[4:]
    keep, take, quotient = factors(parts, step_len[0], cells_total)
    energy[...] = jnp.broadcast_to(quotient, (8, BS))
    for i in range(NSEC):
        for t, (current, applied) in enumerate(((current_a, applied_a), (current_b, applied_b))):
            value = keep * current[i] - take * applied[i]
            hold[t * NSEC + i] = value
            psi[t * NSEC + i] = value.T

    def gram(dims, one, two):
        kw = dict(precision=lax.Precision.HIGHEST, preferred_element_type=F32)
        return lax.dot_general(one, one, dims, **kw) + lax.dot_general(two, two, dims, **kw)

    core = lax.rem(place[0], 2)
    for mine, out in ((core, keep_rho), (1 - core, give_rho)):
        for chip in range(NSEC // 2):
            sector = 2 * chip + mine
            out[chip, 0] = gram(COLS_COLS, hold[sector], hold[NSEC + sector])
            one = hold[inverse[place[0] * 2, sector]]
            two = hold[NSEC + inverse[place[0] * 2 + 1, sector]]
            out[chip, 1] = gram(ROWS_ROWS, one, two)


def finish(cells_total, place, step_size, inverse, parts, currents, applieds):
    rho = jax.ShapeDtypeStruct((NSEC // 2, 2, BS, BS), F32)
    psi = jax.ShapeDtypeStruct((2 * NSEC, BS, BS), F32)
    return pl.pallas_call(
        functools.partial(finish_kernel, cells_total),
        out_shape=(psi, jax.ShapeDtypeStruct((8, BS), F32), rho, rho),
        in_specs=[SMEM] * 3 + [VMEM] * 8,
        out_specs=(VMEM,) * 4,
        scratch_shapes=[pltpu.VMEM(psi.shape, F32)],
        compiler_params=parameters(24),
    )(place, step_size, inverse, *parts, *currents, *applieds)


def fold_kernel(place, mine, other, *outs):
    chips = mine.shape[0]
    for by in range(chips):
        chip = lax.rem(place[0] // 2 + by, chips)
        for n in range(2):
            outs[2 * by + n][...] = mine[chip, n] + other[chip, n]


def fold(place, mine, other):
    chips = mine.shape[0]
    return pl.pallas_call(
        fold_kernel,
        out_shape=(jax.ShapeDtypeStruct((BS, BS), F32),) * (2 * chips),
        in_specs=[SMEM, VMEM, VMEM],
        out_specs=(VMEM,) * (2 * chips),
        compiler_params=parameters(8),
    )(place, mine, other)


def on_device_paired(psi_init, env_left, env_right, coef, source, right_sector, sector_sizes, step_size):
    count = lax.axis_size("blk")
    segments = lax.axis_size("seg")
    line = count // 2
    me = lax.axis_index("blk")
    labels = right_sector[0]
    sizes = sector_sizes[0]
    cells_total = float(NB * BS * BS)

    def swapped(x):
        return lax.ppermute(x, "blk", [(i, i ^ 1) for i in range(count)])

    def shifted(x, by=1):
        return lax.ppermute(x, "blk", [(i, (i + 2 * by) % count) for i in range(count)])

    def handed_on(x, by):
        route = [
            (s * count + i, (s + 1) * count + (i + 2 * by) % count)
            for s in range(segments - 1)
            for i in range(count)
        ]
        return lax.ppermute(x, ("seg", "blk"), route)

    owner = source[0] // (2 * NSEC)
    plane = (owner % 2) ^ (me % 2)
    behind = (me // 2 - owner // 2) % line
    spots = ((plane * line + behind) * (2 * NSEC) + source[0] % (2 * NSEC)).astype(jnp.int32)
    there = ((((1 - plane) * line + behind)) * (2 * NSEC) + source[0] % (2 * NSEC)).astype(jnp.int32)

    mine = (env_left[0], env_right[0], coef[0])
    other = tuple(swapped(x) for x in mine)
    envs = (mine[0], other[0], mine[1], other[1])
    sector = jnp.arange(NSEC, dtype=jnp.int32)
    inverse = jnp.sum(
        jnp.where(labels[:, :, None] == sector[None, None, :], sector[None, :, None], 0), axis=1
    ).astype(jnp.int32)
    tables = (mine[2], other[2], spots, swapped(there), inverse)
    places = [((me - 2 * by) % count).astype(jnp.int32).reshape(1) for by in range(line)]

    own_count = psi_init.shape[1]
    own_ids = me * own_count + jnp.arange(own_count, dtype=jnp.int32)
    begin = psi_init[0] * block_mask(own_ids, sizes, labels.reshape(NB))
    narrow = [begin[t * NSEC : (t + 1) * NSEC].astype(BF) for t in range(2)]
    current = [jnp.swapaxes(begin[t * NSEC : (t + 1) * NSEC], 1, 2) for t in range(2)]
    for iteration in range(ITERS):
        pieces = list(narrow)
        moving = list(narrow)
        for _ in range(line - 1):
            moving = [shifted(x) for x in moving]
            pieces += moving
        full = assemble(pieces + [swapped(x) for x in pieces])
        turned = iteration > 0
        parts = [terms(turned, places[by], tables, full, envs) for by in (*range(1, line), 0)]
        moving = [shifted(relay([], parts[0][t])) for t in range(2)]
        for step in range(1, line - 1):
            moving = [shifted(relay([moving[t]], parts[step][t])) for t in range(2)]
        applied, sums = [None, None], []
        for t in range(2):
            applied[t], one = combine(
                t, places[0], sizes, labels, sums, parts[line - 1][t], moving[t], current[t]
            )
            sums = [one]
        chip = sums[0] + swapped(sums[0])
        sums = [chip] + [shifted(chip, by) for by in range(1, line)]
        if iteration < ITERS - 1:
            for t in range(2):
                current[t], narrow[t] = update(cells_total, step_size, sums, current[t], applied[t])
    psi, energy, keep_rho, give_rho = finish(
        cells_total, places[0], step_size, inverse, sums, current, applied
    )
    folded = fold(places[0], keep_rho, swapped(give_rho))
    density = folded[0]
    for by in range(1, line):
        density = density + shifted(folded[2 * by], by)
    for by in range(line):
        density = density + handed_on(folded[2 * by + 1], by)
    density = density / float(P_SIZE * BS)
    return (psi[None], energy[0, :1], density[None])


def solution(mesh):
    in_specs = (
        P("seg", "blk", None, None),
        P("seg", "blk", None, None, None),
        P("seg", "blk", None, None, None),
        P("seg", "blk", None),
        P("seg", "blk", None),
        P("seg", None, None),
        P("seg", None, None),
        P("seg"),
    )
    out_specs = (P("seg", "blk", None, None), P("seg"), P("seg", "blk", None))
    paired = NB // mesh.shape["blk"] == 2 * NSEC and mesh.shape["blk"] == NSEC
    return jax.shard_map(
        on_device_paired if paired else on_device_general,
        mesh=mesh,
        in_specs=in_specs,
        out_specs=out_specs,
        check_vma=False,
    )
```
